32 devices in a mesh: groups: 2 (over x), expert: 16 (over z, y, core).
Axes of the slice: x: 2, y: 2, z: 4, core: 2. Of those that a mesh axis runs over, the one named last changes fastest.
Arguments:
- tokens: bfloat16 [256, 7168], P(('groups', 'expert')), parts along dimension 0, may hold values from -6 to 6
- expert_ids: int32 [256, 2], P(('groups', 'expert')), parts along dimension 0, may hold values from 0 to 3, as said below
- gate_scores: float32 [256, 2], P(('groups', 'expert')), parts along dimension 0, may hold values from 0.2 to 1
- w_gate_up: bfloat16 [16, 7168, 512], P('expert'), may hold values from -0.0625 to 0.0625
- w_down: bfloat16 [16, 256, 7168], P('expert'), may hold values from -0.1875 to 0.1875
Outputs:
- moe_out: bfloat16 [256, 7168], P(('groups', 'expert')), parts along dimension 0
The draws below stay inside these ranges and needn't reach their ends.
There are 2 independent parts, one for each index of `groups`. The reference program is written for one: setup_inputs(seed, part) draws one part's arguments, and reference() takes and returns one part's arrays. A program takes and returns all parts, laid end to end along the dimension named above; an argument that names none is the same for every part. Nothing has to cross between parts.
Inputs may be any that keep to these rules, and one draw needn't show every extreme that they name: `expert_ids`: each row names 2 different experts. In each aligned block of 8 rows (the rows of one device) no expert is named by more than 8 rows, and one expert is named by exactly 8 rows in every block.
All inputs are finite; a program needn't handle non-finite values.
Results may differ from the reference program's by a relative error of at most 0.0058.
Values may be sent and summed in bfloat16 or wider, within the bound.
A program may use at most 128 MiB of HBM per device.

```python
import math
import jax
import jax.numpy as jnp
from jax import lax

D = 7168
FH = 1024
SPLIT = 4
FH_DEV = 256
ROWS_DEV = 8
EXPERTS = 4
TOP = 2
ROWS = 128
CAP = 8
N_EXPERT = 16


def draw_expert_ids(key, part):
    key_hot, key_perm, key_split = jax.random.split(jax.random.fold_in(key, 11), 3)
    hottest = jax.random.randint(key_hot, (), 0, EXPERTS)
    perm_keys = jax.random.split(key_perm, N_EXPERT)
    others = jax.vmap(lambda subkey: jax.random.permutation(subkey, EXPERTS - 1))(perm_keys)
    ranking = jnp.concatenate([jnp.zeros((N_EXPERT, 1), jnp.int32), (others + 1).astype(jnp.int32)], axis=1)
    ranking = (ranking + hottest) % EXPERTS
    pair_count = EXPERTS // 2
    minor_share = jax.random.randint(key_split, (N_EXPERT, pair_count), 0, CAP // 2 + 1)
    minor_share = jnp.where(jnp.arange(pair_count)[None, :] == 0, 0, minor_share)
    row_index = jnp.arange(ROWS_DEV)[:, None]
    route_index = jnp.arange(TOP)[None, :]
    position = row_index + route_index * ROWS_DEV
    pair_index = position // CAP
    offset = position % CAP
    block_index = jnp.arange(N_EXPERT)[:, None, None]
    major_limit = CAP - minor_share[block_index, pair_index[None, :, :]]
    chosen = 2 * pair_index[None, :, :] + (offset[None, :, :] >= major_limit).astype(jnp.int32)
    drawn_ids = ranking[block_index, chosen]
    return drawn_ids.reshape(N_EXPERT * ROWS_DEV, TOP).astype(jnp.int32)


def steps_of(own_key, shape, cuts, least, top_value):
    loudness = 1.0
    for dim, blocks in cuts:
        steps = jax.random.uniform(jax.random.fold_in(jax.random.fold_in(own_key, 6), dim), (blocks,), jnp.float32, least / len(cuts), top_value / len(cuts))
        loudness = loudness * jnp.repeat(jnp.exp(steps), shape[dim] // blocks).reshape((-1,) + (1,) * (len(shape) - 1 - dim))
    return loudness


def noise(own_key, shape, width, reach, pieces=(), kind=jnp.bfloat16):
    result = width * jax.random.normal(own_key, shape, jnp.float32)
    if pieces:
        result = result * steps_of(own_key, shape, pieces, -0.22, 0.18)
    return jnp.clip(result, -reach, reach).astype(kind)


def setup_inputs(seed: int = 0, part: int = 0) -> dict:
    splits = jax.random.split(jax.random.key(seed), 6)
    part_splits = jax.random.split(jax.random.fold_in(splits[5], part), 6)
    tokens = noise(part_splits[0], (ROWS, D), 1.0, 6.0, ((0, 16),))
    expert_ids = draw_expert_ids(jax.random.fold_in(jax.random.fold_in(splits[5], part), 71), part)
    gate_scores = jnp.clip(jnp.exp(math.log(1.0) - 1.609438 * jax.random.uniform(part_splits[2], (ROWS, TOP), jnp.float32) ** steps_of(part_splits[2], (ROWS, TOP), ((0, 16),), -0.2, 0.2)), 0.2, 1.0)
    w_gate_up = noise(splits[3], (N_EXPERT, D, 2 * FH_DEV), D ** -0.5, 0.0625, ((0, 16),))
    w_down = noise(splits[4], (N_EXPERT, FH_DEV, D), FH ** -0.5, 0.1875, ((0, 16),))
    return dict(tokens=tokens, expert_ids=expert_ids, gate_scores=gate_scores, w_gate_up=w_gate_up, w_down=w_down)


def expert_block(block_tokens, gate_up_part, down_part):
    hidden_width = down_part.shape[0]
    gate_up = jnp.dot(block_tokens, gate_up_part, preferred_element_type=jnp.float32)
    hidden = (jax.nn.silu(gate_up[:, :hidden_width]) * gate_up[:, hidden_width:]).astype(jnp.bfloat16)
    return jnp.dot(hidden, down_part, preferred_element_type=jnp.float32).astype(jnp.bfloat16)


def reference(tokens, expert_ids, gate_scores, w_gate_up, w_down):
    row_count = expert_ids.shape[0]
    route_count = expert_ids.shape[1]
    route_weight = 2.5 * gate_scores / jnp.sum(gate_scores, axis=1, keepdims=True)
    flat_ids = expert_ids.reshape(-1)
    flat_weights = route_weight.reshape(-1)
    capacity_rows = N_EXPERT * CAP
    empty_index = row_count * route_count

    def add_expert(running, expert_index):
        chosen = jnp.nonzero(flat_ids == expert_index, size=capacity_rows, fill_value=empty_index)[0].astype(jnp.int32)
        row_index = chosen // route_count
        block_tokens = jnp.take(tokens, row_index, axis=0, mode="fill", fill_value=0)
        summed = jnp.zeros((capacity_rows, tokens.shape[1]), jnp.float32)
        for share in range(SPLIT):
            slot = expert_index * SPLIT + share
            summed = summed + expert_block(block_tokens, w_gate_up[slot], w_down[slot]).astype(jnp.float32)
        weight_of = jnp.take(flat_weights, chosen, mode="fill", fill_value=0.0)
        contribution = weight_of[:, None] * summed
        running = running.at[row_index].add(contribution, mode="drop")
        return running, None

    start = jnp.zeros((row_count, tokens.shape[1]), jnp.float32)
    running, _ = lax.scan(add_expert, start, jnp.arange(EXPERTS, dtype=jnp.int32))
    return running.astype(jnp.bfloat16)
```

```python
import functools

import jax
import jax.numpy as jnp
from jax import lax
from jax.experimental import pallas as pl
from jax.experimental.pallas import tpu as pltpu
from jax.sharding import PartitionSpec as P

SPLIT = 4
ROUTE_SCALE = 2.5
TILE = 256


def ring_chip(position, chips, folded):
    if not folded:
        return position
    length = chips // 2
    side = position // length
    along = position % length
    return (along + side * (length - 1 - 2 * along)) * 2 + side


def ring_position(chip, chips, folded):
    if not folded:
        return chip
    length = chips // 2
    along = chip // 2
    side = chip % 2
    return along + side * (chips - 1 - 2 * along)


def kernel(n, chunks, folded, tokens_ref, route_ref, wg_hbm, wd_hbm, out_ref,
           x, routes, wg, wd, gate_up, hidden, column, own, to_sib, from_sib, outgoing, incoming,
           wg_sem, wd_sem, ag_send, ag_recv, sib_send, sib_recv,
           rt_send, rt_recv, rts_send, rts_recv, xs_send, xs_recv, rs_send, rs_recv):
    chips = n // 2
    half = chips // 2
    rows, width = tokens_ref.shape
    step = width // chunks
    ring_rows = chips * rows
    hid = wd.shape[0]

    me = lax.axis_index("expert")
    core = me % 2
    pos = ring_position(me // 2, chips, folded)
    right = ring_chip((pos + 1) % chips, chips, folded) * 2 + core
    left = ring_chip((pos + chips - 1) % chips, chips, folded) * 2 + core
    sib = me + 1 - 2 * core
    peer = (right, left)

    wg_copies = [
        pltpu.make_async_copy(wg_hbm.at[0, pl.ds(c * step, step), :],
                              wg.at[pl.ds(c * step, step), :], wg_sem.at[c])
        for c in range(chunks)
    ]
    wd_copies = [
        pltpu.make_async_copy(wd_hbm.at[0, :, pl.ds(c * step, step)],
                              wd.at[:, pl.ds(c * step, step)], wd_sem.at[c])
        for c in range(chunks)
    ]

    barrier = pltpu.get_barrier_semaphore()
    for other in (left, right, sib):
        pl.semaphore_signal(barrier, inc=1, device_id={"expert": other},
                            device_id_type=pl.DeviceIdType.MESH)
    for copy in wg_copies:
        copy.start()
    for copy in wd_copies:
        copy.start()
    pl.semaphore_wait(barrier, 3)

    def remote(src, dst, send, recv, device):
        return pltpu.make_async_remote_copy(
            src_ref=src, dst_ref=dst, send_sem=send, recv_sem=recv,
            device_id={"expert": device}, device_id_type=pl.DeviceIdType.MESH)

    def reach(way, c):
        return half if (c < chunks // 2) == (way == 0) else half - 1

    def slot_of(way, d):
        return d if way == 0 else (chips - d) % chips

    def block(ref, slot, c):
        return ref.at[pl.ds(slot * rows, rows), pl.ds(c * step, step)]

    def route_block(slot):
        return routes.at[pl.ds(slot * rows, rows), :]

    sends = []

    def ag_copy(way, d, c):
        src = (tokens_ref.at[:, pl.ds(c * step, step)] if d == 1
               else block(x, slot_of(way, d - 1), c))
        return remote(src, block(x, slot_of(way, d), c),
                      ag_send.at[way, d - 1, c], ag_recv.at[way, d - 1, c], peer[way])

    def sib_copy(slot, c):
        src = (tokens_ref.at[:, pl.ds(c * step, step)] if slot == 0 else block(x, slot, c))
        return remote(src, block(x, chips + slot, c),
                      sib_send.at[slot, c], sib_recv.at[slot, c], sib)

    def rt_copy(way, d):
        src = route_ref if d == 1 else route_block(slot_of(way, d - 1))
        return remote(src, route_block(slot_of(way, d)),
                      rt_send.at[way, d - 1], rt_recv.at[way, d - 1], peer[way])

    def rts_copy(slot):
        src = route_ref if slot == 0 else route_block(slot)
        return remote(src, route_block(chips + slot), rts_send.at[slot], rts_recv.at[slot], sib)

    def go(copy):
        copy.start()
        sends.append(copy)

    for c in range(chunks):
        for way in range(2):
            go(ag_copy(way, 1, c))
        if c == 0:
            for way in range(2):
                go(rt_copy(way, 1))
    for c in range(chunks):
        go(sib_copy(0, c))
    go(rts_copy(0))
    x[pl.ds(0, rows), :] = tokens_ref[...]
    routes[pl.ds(0, rows), :] = route_ref[...]

    order = [c for pair in zip(range(chunks // 2), range(chunks // 2, chunks)) for c in pair]
    for d in range(1, half + 1):
        for c in order:
            for way in range(2):
                if d > reach(way, c):
                    continue
                ag_copy(way, d, c).wait_recv()
                if d + 1 <= reach(way, c):
                    go(ag_copy(way, d + 1, c))
                go(sib_copy(slot_of(way, d), c))
        for way in range(2):
            far = half if way == 0 else half - 1
            if d <= far:
                rt_copy(way, d).wait_recv()
                if d + 1 <= far:
                    go(rt_copy(way, d + 1))
                go(rts_copy(slot_of(way, d)))

    for index, c in enumerate(order):
        for slot in range(chips):
            sib_copy(slot, c).wait_recv()
        wg_copies[c].wait()
        part = jnp.dot(x[:, pl.ds(c * step, step)], wg[pl.ds(c * step, step), :],
                       preferred_element_type=jnp.float32)
        if index == 0:
            gate_up[...] = part
        else:
            gate_up[...] += part
    for slot in range(chips):
        rts_copy(slot).wait_recv()
    gate = gate_up[:, :hid]
    hidden[...] = (gate / (1.0 + jnp.exp(-gate)) * gate_up[:, hid:]).astype(jnp.bfloat16)
    lane = lax.broadcasted_iota(jnp.int32, routes.shape, 1)
    column[...] = jnp.sum(jnp.where(lane == me // SPLIT, routes[...], 0.0), axis=1, keepdims=True)

    def down(c):
        wd_copies[c].wait()

        def tile(t, carry):
            cols = pl.ds(pl.multiple_of(c * step + t * TILE, TILE), TILE)
            part = column[...] * jnp.dot(hidden[...], wd[:, cols],
                                         preferred_element_type=jnp.float32)
            own[:, cols] = part[:ring_rows]
            to_sib[:, cols] = part[ring_rows:].astype(jnp.bfloat16)
            return carry

        lax.fori_loop(0, step // TILE, tile, 0)

    def exchange(c):
        cols = pl.ds(c * step, step)
        return remote(to_sib.at[:, cols], from_sib.at[:, cols], xs_send.at[c], xs_recv.at[c], sib)

    def rs_copy(way, k, c):
        slot = slot_of(1 - way, k)
        return remote(block(outgoing, slot, c), block(incoming, way * half + k - 1, c),
                      rs_send.at[way, k - 1, c], rs_recv.at[way, k - 1, c], peer[way])

    def piece(slot, c):
        return (pl.ds(slot * rows, rows), pl.ds(c * step, step))

    def heads(c):
        cols = pl.ds(c * step, step)
        exchange(c).wait_recv()
        for way in range(2):
            k = reach(way, c)
            at = piece(slot_of(1 - way, k), c)
            outgoing[at] = (own[at] + from_sib[at].astype(jnp.float32)).astype(jnp.bfloat16)
            go(rs_copy(way, k, c))

    for index, c in enumerate(order):
        down(c)
        go(exchange(c))
        if index:
            heads(order[index - 1])
    heads(order[-1])

    for r in range(1, half + 1):
        for c in order:
            for way in range(2):
                k = reach(way, c) - r
                if k < 1:
                    continue
                rs_copy(way, k + 1, c).wait_recv()
                at = piece(slot_of(1 - way, k), c)
                arrived = piece(way * half + k, c)
                outgoing[at] = (own[at] + from_sib[at].astype(jnp.float32)
                                + incoming[arrived].astype(jnp.float32)).astype(jnp.bfloat16)
                go(rs_copy(way, k, c))
    for c in order:
        at = piece(0, c)
        total = own[at] + from_sib[at].astype(jnp.float32)
        for way in range(2):
            rs_copy(way, 1, c).wait_recv()
            total = total + incoming[piece(way * half, c)].astype(jnp.float32)
        out_ref[:, pl.ds(c * step, step)] = total.astype(jnp.bfloat16)
    for copy in sends:
        copy.wait_send()


def body(n, tokens, expert_ids, gate_scores, w_gate_up, w_down):
    rows, width = tokens.shape
    hid = w_down.shape[1]
    chips = n // 2
    half = chips // 2
    folded = chips == 8
    chunks = 4 if n <= 16 else 2
    weights = ROUTE_SCALE * gate_scores / jnp.sum(gate_scores, axis=1, keepdims=True)
    named = expert_ids[:, :, None] == jnp.arange(128, dtype=jnp.int32)[None, None, :]
    routed = jnp.sum(jnp.where(named, weights[:, :, None], 0.0), axis=1)
    vmem, dma = pltpu.VMEM, pltpu.SemaphoreType.DMA
    bf16, f32 = jnp.bfloat16, jnp.float32
    return pl.pallas_call(
        functools.partial(kernel, n, chunks, folded),
        out_shape=jax.ShapeDtypeStruct((rows, width), bf16),
        in_specs=[
            pl.BlockSpec(memory_space=pltpu.VMEM),
            pl.BlockSpec(memory_space=pltpu.VMEM),
            pl.BlockSpec(memory_space=pl.ANY),
            pl.BlockSpec(memory_space=pl.ANY),
        ],
        out_specs=pl.BlockSpec(memory_space=pltpu.VMEM),
        scratch_shapes=[
            vmem((n * rows, width), bf16),
            vmem((n * rows, 128), f32),
            vmem((width, 2 * hid), bf16),
            vmem((hid, width), bf16),
            vmem((n * rows, 2 * hid), f32),
            vmem((n * rows, hid), bf16),
            vmem((n * rows, 1), f32),
            vmem((chips * rows, width), f32),
            vmem((chips * rows, width), bf16),
            vmem((chips * rows, width), bf16),
            vmem((chips * rows, width), bf16),
            vmem((2 * half * rows, width), bf16),
            dma((chunks,)), dma((chunks,)),
            dma((2, half, chunks)), dma((2, half, chunks)),
            dma((chips, chunks)), dma((chips, chunks)),
            dma((2, half)), dma((2, half)),
            dma((chips,)), dma((chips,)),
            dma((chunks,)), dma((chunks,)),
            dma((2, half, chunks)), dma((2, half, chunks)),
        ],
        compiler_params=pltpu.CompilerParams(collective_id=0, has_side_effects=True),
        name="routed_experts",
    )(tokens, routed, w_gate_up, w_down)


def solution(mesh):
    in_specs = (
        P(("groups", "expert"), None),
        P(("groups", "expert"), None),
        P(("groups", "expert"), None),
        P("expert", None, None),
        P("expert", None, None),
    )
    out_specs = P(("groups", "expert"), None)
    return jax.shard_map(
        functools.partial(body, mesh.shape["expert"]),
        mesh=mesh, in_specs=in_specs, out_specs=out_specs, check_vma=False)
```
